32 devices in a mesh: sweep: 2 (over x), seq: 16 (over z, y, core).
Axes of the slice: x: 2, y: 2, z: 4, core: 2. Of those that a mesh axis runs over, the one named last changes fastest.
Arguments:
- queries: bfloat16 [6144, 4096], P(('sweep', 'seq')), parts along dimension 0, may hold values from -6 to 6
- keys: bfloat16 [6144, 4096], P(('sweep', 'seq')), parts along dimension 0, may hold values from -6 to 6
- values: bfloat16 [6144, 4096], P(('sweep', 'seq')), parts along dimension 0, may hold values from -6 to 6
- out_grad: bfloat16 [6144, 4096], P(('sweep', 'seq')), parts along dimension 0, may hold values from -6 to 6
- doc_blocks: int32 [8], P('sweep'), parts along dimension 0, may hold values from 1 to 10, 24 in all
Outputs:
- attn_out: bfloat16 [6144, 4096], P(('sweep', 'seq')), parts along dimension 0
- grad_q: bfloat16 [6144, 4096], P(('sweep', 'seq')), parts along dimension 0
- grad_k: bfloat16 [6144, 4096], P(('sweep', 'seq')), parts along dimension 0
- grad_v: bfloat16 [6144, 4096], P(('sweep', 'seq')), parts along dimension 0
The draws below stay inside these ranges and needn't reach their ends.
There are 2 independent parts, one for each index of `sweep`. The reference program is written for one: setup_inputs(seed, part) draws one part's arguments, and reference() takes and returns one part's arrays. A program takes and returns all parts, laid end to end along the dimension named above; each array names one. Nothing has to cross between parts.
Inputs may be any that keep to these rules, and one draw needn't show every extreme that they name: `doc_blocks`: the lengths sum to 24 and the longest is exactly 10, so a document touches at most 8 consecutive blocks of 192 tokens.
All inputs are finite; a program needn't handle non-finite values.
Results may differ from the reference program's by a relative error of at most 0.012.
Values may be sent and summed in bfloat16 or wider, within the bound.
No kernel may reach another device: no remote copies, remote signals or barrier semaphores. Data moves between devices by JAX's collectives and lax.ppermute only.
A program may use at most 64 MiB of HBM per device.

```python
import math
import jax
import jax.numpy as jnp
import numpy as np
from jax import lax

H = 32
DH = 128
TOK_DEV = 192
TOKENS = 3072
BLOCKS = 24
DOC_MOST = 10
DOCS = 4
N_SEQ = 16


def level_of(key, shape, pieces, low, high):
    level, own = 1.0, jax.random.fold_in(key, 6)
    for axis_at, shards_of in pieces:
        steps = jnp.exp(jax.random.uniform(jax.random.fold_in(own, axis_at), (shards_of,), jnp.float32, low / len(pieces), high / len(pieces)))
        level = level * jnp.repeat(steps, shape[axis_at] // shards_of).reshape([-1 if axis == axis_at else 1 for axis in range(len(shape))])
    return level


def length_profile(count, total, limit, lean):
    loads = [(1 << 20) // math.isqrt(grade ** lean) + 1 for grade in range(2, count + 1)]
    rest, holding = total - limit - (count - 1), [1] * (count - 1)
    while rest > 0:
        movable = [i for i in range(count - 1) if holding[i] < limit]
        pool, remaining = sum([loads[i] for i in movable]), rest
        for i in movable:
            addition = min(limit - holding[i], max(1, remaining * loads[i] // pool), rest)
            holding[i] = holding[i] + addition
            rest = rest - addition
    return np.array([limit] + holding)


def uneven(rng, count, total, limit, slope):
    if count == 2:
        one = jax.random.randint(rng, (), max(1, total - limit), min(limit, total - 1) + 1)
        return jnp.stack([one, total - one])
    sizes = jnp.asarray(length_profile(count, total, limit, slope), jnp.int32)
    pairs = (count - 1) // 2
    source_of, taker = sizes[1:1 + 2 * pairs:2], sizes[2:2 + 2 * pairs:2]
    margin = jnp.minimum(source_of - 1, limit - taker)
    passed = jax.random.randint(jax.random.fold_in(rng, 1), (pairs,), 0, 1 << 20) % (margin + 1)
    sizes = sizes.at[1:1 + 2 * pairs:2].set(source_of - passed).at[2:2 + 2 * pairs:2].set(taker + passed)
    return sizes[jax.random.permutation(jax.random.fold_in(rng, 2), count)]


def normal_values(own_key, shape, spread, reach, split=(), kind=jnp.bfloat16):
    entries = jax.random.normal(own_key, shape, jnp.float32) * spread
    if len(split) > 0:
        entries = level_of(own_key, shape, split, -0.22, 0.18) * entries
    return jnp.clip(entries, min=-reach, max=reach).astype(kind)


def setup_inputs(seed: int = 0, part: int = 0) -> dict:
    splits = jax.random.split(jax.random.key(seed), 6)
    part_splits = jax.random.split(jax.random.fold_in(splits[5], part), 6)
    return {
        "queries": normal_values(part_splits[0], (TOKENS, H * DH), 1.0, 6.0, ((0, 16),)),
        "keys": normal_values(part_splits[1], (TOKENS, H * DH), 1.0, 6.0, ((0, 16),)),
        "values": normal_values(part_splits[2], (TOKENS, H * DH), 1.0, 6.0, ((0, 16),)),
        "out_grad": normal_values(part_splits[3], (TOKENS, H * DH), 1.0, 6.0, ((0, 16),)),
        "doc_blocks": uneven(part_splits[4], DOCS, BLOCKS, DOC_MOST, 2).astype(jnp.int32),
    }


def doc_number(spots_listing, doc_ends):
    counted = lax.optimization_barrier(jnp.sum((spots_listing[:, None] >= doc_ends[None, :]).astype(jnp.int32), axis=1)).astype(jnp.int32)
    return jnp.where(spots_listing < 0, jnp.int32(-1), counted).astype(jnp.int32)

def upcast_float(array):
    return array.astype(jnp.float32)

def reference(queries, keys, values, out_grad, doc_blocks):
    out_scale = 1.0 / math.sqrt(DH * 32 * DOC_MOST)
    doc_ends = (jnp.cumsum(doc_blocks).astype(jnp.int32) * 128).astype(jnp.int32)

    def split_blocks(array):
        return array.reshape(N_SEQ, TOK_DEV, H, DH)
    indices = jnp.arange(N_SEQ, dtype=jnp.int32)
    blocks = (split_blocks(queries), split_blocks(keys), split_blocks(values), split_blocks(out_grad), indices)
    causal = jnp.arange(TOK_DEV)[:, None] >= jnp.arange(TOK_DEV)[None, :]

    def layout(index):
        first_pos = (index * TOK_DEV).astype(jnp.int32)
        spots_listing = (first_pos + jnp.arange(TOK_DEV, dtype=jnp.int32)).astype(jnp.int32)
        doc_ids = doc_number(spots_listing, doc_ends)
        edge_pos = jnp.stack([first_pos - 1, first_pos + TOK_DEV]).astype(jnp.int32)
        edge_docs = doc_number(edge_pos, doc_ends)
        return (doc_ids, edge_docs[0], edge_docs[1])

    def backward_step(incoming_derivative, items):
        query_block, key_block, payload_tile, derivative_tile, index = items
        doc_ids, prev_doc, next_doc = layout(index)
        head_rows = doc_ids == doc_ids[0]
        picked_lines = jnp.where(head_rows[:, None, None], query_block, jnp.zeros((), query_block.dtype))
        channel_derivative = jnp.einsum('oni,onw->niw', upcast_float(picked_lines), upcast_float(derivative_tile)).astype(jnp.bfloat16)
        flag = (doc_ids[0] != next_doc).astype(jnp.float32)
        new_grad = (upcast_float(channel_derivative) + (1.0 - flag) * upcast_float(incoming_derivative)).astype(jnp.bfloat16)
        return (new_grad, incoming_derivative)
    start_state = jnp.zeros((H, DH, DH), jnp.bfloat16)
    _, grad_states = lax.scan(backward_step, start_state, blocks, reverse=True)

    def forward_step(state_in, items):
        query_block, key_block, payload_tile, derivative_tile, index, incoming_derivative = items
        doc_ids, prev_doc, next_doc = layout(index)
        allowed = (doc_ids[:, None] == doc_ids[None, :]) & causal
        tail_rows = doc_ids == doc_ids[TOK_DEV - 1]
        picked_lines = jnp.where(tail_rows[:, None, None], key_block, jnp.zeros((), key_block.dtype))
        closing_memory = jnp.einsum('oni,onw->niw', upcast_float(picked_lines), upcast_float(payload_tile)).astype(jnp.bfloat16)
        flag = (doc_ids[TOK_DEV - 1] != prev_doc).astype(jnp.float32)
        state_block = upcast_float(state_in)
        backward_block = upcast_float(incoming_derivative)
        input_selector = (doc_ids == prev_doc)[:, None, None]
        output_selector = (doc_ids == next_doc)[:, None, None]
        scores = jnp.einsum('thd,shd->hts', upcast_float(query_block), upcast_float(key_block))
        probs = upcast_float(jnp.where(allowed[None], scores, 0.0).astype(jnp.bfloat16))
        dscores = jnp.einsum('thd,shd->hts', upcast_float(derivative_tile), upcast_float(payload_tile))
        dprobs = upcast_float(jnp.where(allowed[None], dscores, 0.0).astype(jnp.bfloat16))
        attention_core = jnp.einsum('hts,shd->thd', probs, upcast_float(payload_tile))
        attention_core = attention_core + jnp.where(input_selector, jnp.einsum('xra,ras->xrs', upcast_float(query_block), state_block), 0.0)
        query_gradient = jnp.einsum('hts,shd->thd', dprobs, upcast_float(key_block))
        query_gradient = query_gradient + jnp.where(input_selector, jnp.einsum('jox,odx->jod', upcast_float(derivative_tile), state_block), 0.0)
        key_gradient = jnp.einsum('hts,thd->shd', dprobs, upcast_float(query_block))
        key_gradient = key_gradient + jnp.where(output_selector, jnp.einsum('nom,ogm->nog', upcast_float(payload_tile), backward_block), 0.0)
        value_gradient = jnp.einsum('hts,thd->shd', probs, upcast_float(derivative_tile))
        value_gradient = value_gradient + jnp.where(output_selector, jnp.einsum('zlw,lwi->zli', upcast_float(key_block), backward_block), 0.0)
        results = tuple(((out_scale * item).astype(jnp.bfloat16) for item in (attention_core, query_gradient, key_gradient, value_gradient)))
        new_state = (upcast_float(closing_memory) + (1.0 - flag) * state_block).astype(jnp.bfloat16)
        return (new_state, results)
    _, outputs = lax.scan(forward_step, start_state, blocks + (grad_states,))
    flat = tuple((item.reshape(TOKENS, H * DH) for item in outputs))
    return (flat[0], flat[1], flat[2], flat[3])
```

```python
import functools
import math

import jax
import jax.numpy as jnp
from jax import lax
from jax.experimental import pallas as pl
from jax.experimental.pallas import tpu as pltpu
from jax.sharding import PartitionSpec as P

DH = 128
UNIT = 128
LONGEST = 10
F32 = jnp.float32
BF16 = jnp.bfloat16


def doc_of(pos, doc_ref, docs):
    count = jnp.int32(0)
    end = jnp.int32(0)
    for d in range(docs):
        end = end + doc_ref[d] * UNIT
        count = count + (pos >= end).astype(jnp.int32)
    return jnp.where(pos < 0, jnp.int32(-1), count)


def edges(pos_ref, doc_ref, rows, docs):
    first = pos_ref[0] * rows
    start = jnp.int32(0)
    stop = jnp.int32(1 << 30)
    end = jnp.int32(0)
    for d in range(docs):
        end = end + doc_ref[d] * UNIT
        start = jnp.where(end <= first + (rows - 1), end, start)
        stop = jnp.minimum(stop, jnp.where(end > first, end, jnp.int32(1 << 30)))
    return start - first, stop - first


def dot_tt(a, b):
    return lax.dot_general(a, b, (((0,), (0,)), ((), ())), preferred_element_type=F32)


def dot_nt(a, b):
    return lax.dot_general(a, b, (((1,), (1,)), ((), ())), preferred_element_type=F32)


def dot_nn(a, b):
    return lax.dot_general(a, b, (((1,), (0,)), ((), ())), preferred_element_type=F32)


def tails_kernel(pos_ref, doc_ref, q_ref, k_ref, v_ref, g_ref, keep_ref, send_ref, w_ref, *, docs, heads):
    rows = q_ref.shape[0]
    dev = pos_ref[0]
    core = lax.rem(dev, 2)
    start, stop = edges(pos_ref, doc_ref, rows, docs)
    row = lax.broadcasted_iota(jnp.int32, (rows, DH), 0)
    in_tail = row >= start
    in_head = row < stop

    @pl.when(pl.program_id(0) == 0)
    def _():
        chip = dev - core

        def key(u):
            pos = jnp.where(core == 0, rows * (chip + 2 - u) - 1, rows * (chip + u))
            return doc_of(pos, doc_ref, docs)

        k0, k1, k2, k4 = key(0), key(1), key(2), key(4)
        same = (k1 == k0, k2 == k0, k4 == k2, k4 == k0, k2 == k1)
        for i, flag in enumerate(same):
            w_ref[i] = flag.astype(F32)
        for i in range(len(same), 8):
            w_ref[i] = jnp.float32(0)

    zero = jnp.zeros((), BF16)
    for i in range(heads):
        cols = pl.ds(i * DH, DH)
        tail = dot_tt(jnp.where(in_tail, k_ref[:, cols], zero), v_ref[:, cols]).astype(BF16)
        head = dot_tt(jnp.where(in_head, q_ref[:, cols], zero), g_ref[:, cols]).astype(BF16)
        keep_ref[i] = jnp.where(core == 0, tail, head)
        send_ref[i] = jnp.where(core == 0, head, tail)


def local_kernel(pos_ref, doc_ref, q_ref, k_ref, v_ref, g_ref, o_ref, dq_ref, dk_ref, dv_ref, mask_ref, *, docs, heads, scale):
    rows = q_ref.shape[0]

    @pl.when(pl.program_id(0) == 0)
    def _():
        start, _ = edges(pos_ref, doc_ref, rows, docs)
        t = lax.broadcasted_iota(jnp.int32, (rows, rows), 0)
        s = lax.broadcasted_iota(jnp.int32, (rows, rows), 1)
        allowed = (s <= t) & ((t < start) | (s >= start))
        mask_ref[...] = allowed.astype(F32)

    allowed = mask_ref[...] > 0
    for i in range(heads):
        cols = pl.ds(i * DH, DH)
        q, k, v, g = q_ref[:, cols], k_ref[:, cols], v_ref[:, cols], g_ref[:, cols]
        probs = jnp.where(allowed, dot_nt(q, k), 0.0).astype(BF16)
        dprobs = jnp.where(allowed, dot_nt(g, v), 0.0).astype(BF16)
        o_ref[:, cols] = (scale * dot_nn(probs, v)).astype(BF16)
        dq_ref[:, cols] = (scale * dot_nn(dprobs, k)).astype(BF16)
        dk_ref[:, cols] = (scale * dot_tt(dprobs, q)).astype(BF16)
        dv_ref[:, cols] = (scale * dot_tt(probs, g)).astype(BF16)


def final_kernel(pos_ref, doc_ref, q_ref, k_ref, v_ref, g_ref, mine_ref, other_ref, o_in, dq_in, dk_in, dv_in, o_ref, dq_ref, dk_ref, dv_ref, *, docs, heads, scale):
    rows = q_ref.shape[0]
    dev = pos_ref[0]
    forward = lax.rem(dev, 2) == 0
    first = dev * rows
    prev_doc = doc_of(first - 1, doc_ref, docs)
    next_doc = doc_of(first + rows, doc_ref, docs)
    first_doc = doc_of(first, doc_ref, docs)
    last_doc = doc_of(first + (rows - 1), doc_ref, docs)
    start, stop = edges(pos_ref, doc_ref, rows, docs)
    row = lax.broadcasted_iota(jnp.int32, (rows, DH), 0)
    into = jnp.where(first_doc == prev_doc, stop, 0)
    onto = jnp.where(last_doc == next_doc, start, rows)
    reads = row < into
    feeds = row >= onto
    for i in range(heads):
        cols = pl.ds(i * DH, DH)
        q, k, v, g = q_ref[:, cols], k_ref[:, cols], v_ref[:, cols], g_ref[:, cols]
        state = jnp.where(forward, mine_ref[i], other_ref[i])
        back = jnp.where(forward, other_ref[i], mine_ref[i])
        o_ref[:, cols] = (o_in[:, cols].astype(F32) + jnp.where(reads, scale * dot_nn(q, state), 0.0)).astype(BF16)
        dq_ref[:, cols] = (dq_in[:, cols].astype(F32) + jnp.where(reads, scale * dot_nt(g, state), 0.0)).astype(BF16)
        dk_ref[:, cols] = (dk_in[:, cols].astype(F32) + jnp.where(feeds, scale * dot_nt(v, back), 0.0)).astype(BF16)
        dv_ref[:, cols] = (dv_in[:, cols].astype(F32) + jnp.where(feeds, scale * dot_nn(k, back), 0.0)).astype(BF16)


def on_device(queries, keys, values, out_grad, doc_blocks):
    rows, width = queries.shape
    n_heads = width // DH
    docs = doc_blocks.shape[0]
    devices = lax.axis_size("seq")
    scale = 1.0 / math.sqrt(DH * n_heads * LONGEST)
    dev = lax.axis_index("seq").astype(jnp.int32).reshape(1)
    args = (queries, keys, values, out_grad)
    smem = pl.BlockSpec(memory_space=pltpu.SMEM)
    params = pltpu.CompilerParams(dimension_semantics=("arbitrary",))
    hb = 2

    def wide(off):
        return pl.BlockSpec((rows, hb * DH), lambda i: (0, i + off // hb))

    square = pl.BlockSpec((hb, DH, DH), lambda i: (i, 0, 0))

    def tails(lo, n):
        return pl.pallas_call(
            functools.partial(tails_kernel, docs=docs, heads=hb),
            grid=(n // hb,),
            in_specs=[smem, smem] + [wide(lo)] * 4,
            out_specs=[square, square, smem],
            out_shape=[jax.ShapeDtypeStruct((n, DH, DH), BF16)] * 2 + [jax.ShapeDtypeStruct((8,), F32)],
            compiler_params=params,
            cost_estimate=pl.CostEstimate(flops=4 * n * rows * DH * DH, transcendentals=0, bytes_accessed=n * DH * (8 * rows + 4 * DH)),
            name="tails",
        )(dev, doc_blocks, *args)

    def local(lo, n):
        return pl.pallas_call(
            functools.partial(local_kernel, docs=docs, heads=hb, scale=scale),
            grid=(n // hb,),
            in_specs=[smem, smem] + [wide(lo)] * 4,
            out_specs=[wide(0)] * 4,
            out_shape=[jax.ShapeDtypeStruct((rows, n * DH), BF16)] * 4,
            scratch_shapes=[pltpu.VMEM((rows, rows), F32)],
            compiler_params=params,
            cost_estimate=pl.CostEstimate(flops=12 * n * rows * rows * DH, transcendentals=0, bytes_accessed=16 * n * DH * rows),
            name="local",
        )(dev, doc_blocks, *args)

    def final(lo, n, mine, other, partial, outs):
        aliased = [] if outs is None else list(outs)
        keep = [pl.BlockSpec(memory_space=pl.ANY)] * len(aliased)
        body = functools.partial(final_kernel, docs=docs, heads=hb, scale=scale)
        if aliased:
            inner = body

            def body(*refs):
                inner(*refs[:12], *refs[16:])

        return pl.pallas_call(
            body,
            grid=(n // hb,),
            in_specs=[smem, smem] + [wide(lo)] * 4 + [square] * 2 + [wide(0)] * 4 + keep,
            out_specs=[wide(lo)] * 4,
            out_shape=[jax.ShapeDtypeStruct((rows, width), BF16)] * 4,
            input_output_aliases={12 + i: i for i in range(len(aliased))},
            compiler_params=params,
            cost_estimate=pl.CostEstimate(flops=8 * n * rows * DH * DH, transcendentals=0, bytes_accessed=24 * n * DH * rows),
            name="final",
        )(dev, doc_blocks, *args, mine, other, *partial, *aliased)

    def across(x):
        return lax.ppermute(x, "seq", [(i, i ^ 1) for i in range(devices)])

    def along(x, by):
        pairs = [(i, i + by if i % 2 == 0 else i - by) for i in range(devices)]
        return lax.ppermute(x, "seq", [(i, j) for i, j in pairs if 0 <= j < devices])

    def fma(base, w, x):
        return (base.astype(F32) + w * x.astype(F32)).astype(BF16)

    n_x = 18
    sizes = ((0, n_x), (n_x, n_heads - n_x))
    keep_x, send_x, w = tails(*sizes[0])
    keep_w, send_w, _ = tails(*sizes[1])
    total_x = fma(across(send_x), w[0], keep_x)
    total_w = fma(across(send_w), w[0], keep_w)
    part_x = local(*sizes[0])
    part_w = local(*sizes[1])
    near_x = along(total_x, 2)
    far_w = along(total_w, 4)
    gathered_w = fma(total_w, w[3], far_w)
    near_w = along(gathered_w, 2)
    near_x, _ = lax.optimization_barrier((near_x, gathered_w))
    gathered_x = fma(total_x, w[1], near_x)
    far_x = along(gathered_x, 4)
    mine_x = fma(near_x, w[2], far_x)
    mine_w = fma(near_w, w[2], far_w)
    other_x = across(fma(keep_x, w[4], mine_x))
    other_w = across(fma(keep_w, w[4], mine_w))
    outs = final(*sizes[0], mine_x, other_x, part_x, None)
    outs = final(*sizes[1], mine_w, other_w, part_w, outs)
    return tuple(outs)


def solution(mesh):
    spec = P(("sweep", "seq"), None)
    return jax.shard_map(
        on_device,
        mesh=mesh,
        in_specs=(spec, spec, spec, spec, P("sweep")),
        out_specs=(spec, spec, spec, spec),
        check_vma=False,
    )
```

```python
import functools
import math

import jax
import jax.numpy as jnp
from jax import lax
from jax.experimental import pallas as pl
from jax.experimental.pallas import tpu as pltpu
from jax.sharding import PartitionSpec as P

DH = 128
UNIT = 128
LONGEST = 10
N_X = 18
N_GAP = 4
F32 = jnp.float32
BF16 = jnp.bfloat16


def doc_of(pos, doc_ref, docs):
    count = jnp.int32(0)
    end = jnp.int32(0)
    for d in range(docs):
        end = end + doc_ref[d] * UNIT
        count = count + (pos >= end).astype(jnp.int32)
    return jnp.where(pos < 0, jnp.int32(-1), count)


def edges(pos_ref, doc_ref, rows, docs):
    first = pos_ref[0] * rows
    start = jnp.int32(0)
    stop = jnp.int32(1 << 30)
    end = jnp.int32(0)
    for d in range(docs):
        end = end + doc_ref[d] * UNIT
        start = jnp.where(end <= first + (rows - 1), end, start)
        stop = jnp.minimum(stop, jnp.where(end > first, end, jnp.int32(1 << 30)))
    return start - first, stop - first


def dot_tt(a, b):
    return lax.dot_general(a, b, (((0,), (0,)), ((), ())), preferred_element_type=F32)


def dot_nt(a, b):
    return lax.dot_general(a, b, (((1,), (1,)), ((), ())), preferred_element_type=F32)


def dot_nn(a, b):
    return lax.dot_general(a, b, (((1,), (0,)), ((), ())), preferred_element_type=F32)


def tails_of(pos_ref, doc_ref, q_ref, k_ref, v_ref, g_ref, keep_ref, send_ref, lo, sizes, docs, ready=None):
    rows = q_ref.shape[0]
    even = lax.rem(pos_ref[0], 2) == 0
    start, stop = edges(pos_ref, doc_ref, rows, docs)
    row = lax.broadcasted_iota(jnp.int32, (rows, DH), 0)
    in_tail = row >= start
    in_head = row < stop
    zero = jnp.zeros((), BF16)
    at = 0
    for c, size in enumerate(sizes):
        if ready is not None:
            ready(c)
        for i in range(at, at + size):
            cols = pl.ds((lo + i) * DH, DH)
            tail = dot_tt(jnp.where(in_tail, k_ref[:, cols], zero), v_ref[:, cols]).astype(BF16)
            head = dot_tt(jnp.where(in_head, q_ref[:, cols], zero), g_ref[:, cols]).astype(BF16)
            keep_ref[i] = jnp.where(even, tail, head)
            send_ref[i] = jnp.where(even, head, tail)
        at += size


def open_kernel(pos_ref, doc_ref, q_hbm, k_hbm, v_hbm, g_hbm, q_ref, k_ref, v_ref, g_ref, keep_ref, send_ref, w_ref, sems, *, docs, sizes):
    rows, width = q_ref.shape
    dev = pos_ref[0]
    core = lax.rem(dev, 2)
    arrays = ((k_hbm, k_ref), (v_hbm, v_ref), (q_hbm, q_ref), (g_hbm, g_ref))
    rest = width // DH - sum(sizes)
    copies = []
    at = 0
    for c, size in enumerate((*sizes, rest)):
        cols = pl.ds(at * DH, size * DH)
        group = [pltpu.make_async_copy(src.at[:, cols], dst.at[:, cols], sems.at[c, a]) for a, (src, dst) in enumerate(arrays)]
        for cp in group:
            cp.start()
        copies.append(group)
        at += size
    chip = dev - core

    def key(u):
        pos = jnp.where(core == 0, rows * (chip + 2 - u) - 1, rows * (chip + u))
        return doc_of(pos, doc_ref, docs)

    k0, k1, k2, k4 = key(0), key(1), key(2), key(4)
    same = (k1 == k0, k2 == k0, k4 == k2, k4 == k0, k2 == k1)
    for i, flag in enumerate(same):
        w_ref[i] = flag.astype(F32)
    for i in range(len(same), 8):
        w_ref[i] = jnp.float32(0)

    def ready(c):
        for cp in copies[c]:
            cp.wait()

    tails_of(pos_ref, doc_ref, q_ref, k_ref, v_ref, g_ref, keep_ref, send_ref, 0, sizes, docs, ready)
    ready(len(sizes))


def tails_kernel(pos_ref, doc_ref, q_ref, k_ref, v_ref, g_ref, keep_ref, send_ref, *, docs, lo, n):
    tails_of(pos_ref, doc_ref, q_ref, k_ref, v_ref, g_ref, keep_ref, send_ref, lo, (n,), docs)


def local_kernel(pos_ref, doc_ref, q_ref, k_ref, v_ref, g_ref, o_ref, dq_ref, dk_ref, dv_ref, *, docs, lo, n, scale, unroll):
    rows = q_ref.shape[0]
    start, _ = edges(pos_ref, doc_ref, rows, docs)
    t = lax.broadcasted_iota(jnp.int32, (rows, rows), 0)
    s = lax.broadcasted_iota(jnp.int32, (rows, rows), 1)
    allowed = (s <= t) & ((t < start) | (s >= start))

    def step(j, carry):
        for u in range(unroll):
            i = j * unroll + u
            src = pl.ds(pl.multiple_of((lo + i) * DH, DH), DH)
            dst = pl.ds(pl.multiple_of(i * DH, DH), DH)
            q, k, v, g = q_ref[:, src], k_ref[:, src], v_ref[:, src], g_ref[:, src]
            probs = jnp.where(allowed, dot_nt(q, k), 0.0).astype(BF16)
            dprobs = jnp.where(allowed, dot_nt(g, v), 0.0).astype(BF16)
            o_ref[:, dst] = (scale * dot_nn(probs, v)).astype(BF16)
            dq_ref[:, dst] = (scale * dot_nn(dprobs, k)).astype(BF16)
            dk_ref[:, dst] = (scale * dot_tt(dprobs, q)).astype(BF16)
            dv_ref[:, dst] = (scale * dot_tt(probs, g)).astype(BF16)
        return carry

    lax.fori_loop(0, n // unroll, step, 0)


def final_kernel(pos_ref, doc_ref, q_ref, k_ref, v_ref, g_ref, mine_ref, other_ref, parts, outs, bufs, sems, *, docs, lo, sizes, scale):
    rows = q_ref.shape[0]
    dev = pos_ref[0]
    forward = lax.rem(dev, 2) == 0
    first = dev * rows
    prev_doc = doc_of(first - 1, doc_ref, docs)
    next_doc = doc_of(first + rows, doc_ref, docs)
    first_doc = doc_of(first, doc_ref, docs)
    last_doc = doc_of(first + (rows - 1), doc_ref, docs)
    start, stop = edges(pos_ref, doc_ref, rows, docs)
    row = lax.broadcasted_iota(jnp.int32, (rows, DH), 0)
    into = jnp.where(first_doc == prev_doc, stop, 0)
    onto = jnp.where(last_doc == next_doc, start, rows)
    reads = row < into
    feeds = row >= onto
    copies = []
    at = 0
    for c, size in enumerate(sizes):
        for i in range(at, at + size):
            cols = pl.ds(i * DH, DH)
            src = pl.ds((lo + i) * DH, DH)
            q, k, v, g = q_ref[:, src], k_ref[:, src], v_ref[:, src], g_ref[:, src]
            state = jnp.where(forward, mine_ref[i], other_ref[i])
            back = jnp.where(forward, other_ref[i], mine_ref[i])
            terms = ((reads, dot_nn(q, state)), (reads, dot_nt(g, state)), (feeds, dot_nt(v, back)), (feeds, dot_nn(k, back)))
            piece, rel = 0, i
            while rel * DH >= parts[piece].shape[1]:
                rel -= parts[piece].shape[1] // DH
                piece += 4
            inner = pl.ds(rel * DH, DH)
            for a, (mask, term) in enumerate(terms):
                bufs[a][:, cols] = (parts[piece + a][:, inner].astype(F32) + jnp.where(mask, scale * term, 0.0)).astype(BF16)
        for a in range(4):
            cp = pltpu.make_async_copy(
                bufs[a].at[:, pl.ds(at * DH, size * DH)],
                outs[a].at[:, pl.ds((lo + at) * DH, size * DH)],
                sems.at[c, a],
            )
            cp.start()
            copies.append(cp)
        at += size
    for cp in copies:
        cp.wait()


def plus_kernel(flag_ref, base_ref, x_ref, out_ref, *, which):
    flag = jnp.full(base_ref.shape[1:], flag_ref[which], F32).astype(BF16)
    for i in range(base_ref.shape[0]):
        out_ref[i] = base_ref[i] + flag * x_ref[i]


def close_kernel(flag_ref, near_ref, far_ref, keep_ref, mine_ref, pass_ref, *, one, two):
    flag = jnp.full(near_ref.shape[1:], flag_ref[one], F32).astype(BF16)
    flag2 = jnp.full(near_ref.shape[1:], flag_ref[two], F32).astype(BF16)
    for i in range(near_ref.shape[0]):
        mine = near_ref[i] + flag * far_ref[i]
        mine_ref[i] = mine
        pass_ref[i] = keep_ref[i] + flag2 * mine


def split(n, size):
    return (size,) * (n // size) + ((n % size,) if n % size else ())


def on_device(queries, keys, values, out_grad, doc_blocks):
    rows, width = queries.shape
    n_heads = width // DH
    docs = doc_blocks.shape[0]
    devices = lax.axis_size("seq")
    scale = 1.0 / math.sqrt(DH * n_heads * LONGEST)
    dev = lax.axis_index("seq").astype(jnp.int32).reshape(1)
    smem = pl.BlockSpec(memory_space=pltpu.SMEM)
    vmem = pl.BlockSpec(memory_space=pltpu.VMEM)
    hbm = pl.BlockSpec(memory_space=pltpu.HBM)
    params = pltpu.CompilerParams(vmem_limit_bytes=24 << 20)
    cost = pl.CostEstimate(flops=1024, transcendentals=0, bytes_accessed=1024)

    def shaped(*shape):
        return jax.ShapeDtypeStruct(shape, BF16)

    def opened(n):
        sizes = split(n, 4)
        out = pl.pallas_call(
            functools.partial(open_kernel, docs=docs, sizes=sizes),
            in_specs=[smem, smem] + [hbm] * 4,
            out_specs=[vmem] * 6 + [smem],
            out_shape=[shaped(rows, width)] * 4 + [shaped(n, DH, DH)] * 2 + [jax.ShapeDtypeStruct((8,), F32)],
            scratch_shapes=[pltpu.SemaphoreType.DMA((len(sizes) + 1, 4))],
            compiler_params=pltpu.CompilerParams(vmem_limit_bytes=46 << 20),
            cost_estimate=cost,
            name="opened",
        )(dev, doc_blocks, queries, keys, values, out_grad)
        return out[:4], out[4], out[5], out[6]

    def tails(blocks, lo, n):
        return pl.pallas_call(
            functools.partial(tails_kernel, docs=docs, lo=lo, n=n),
            in_specs=[smem, smem] + [vmem] * 4,
            out_specs=[vmem] * 2,
            out_shape=[shaped(n, DH, DH)] * 2,
            compiler_params=params,
            cost_estimate=cost,
            name="tails",
        )(dev, doc_blocks, *blocks)

    def local(blocks, lo, n, flops=1024):
        return pl.pallas_call(
            functools.partial(local_kernel, docs=docs, lo=lo, n=n, scale=scale, unroll=2),
            in_specs=[smem, smem] + [vmem] * 4,
            out_specs=[vmem] * 4,
            out_shape=[shaped(rows, n * DH)] * 4,
            compiler_params=params,
            cost_estimate=pl.CostEstimate(flops=flops, transcendentals=0, bytes_accessed=1024),
            name="local",
        )(dev, doc_blocks, *blocks)

    def final(blocks, lo, n, mine, other, parts, outs):
        aliased = [] if outs is None else list(outs)
        sizes = split(n, 4)
        first_alias = 8 + len(parts)

        def body(*refs):
            ins, rest = refs[:first_alias], refs[first_alias + len(aliased) :]
            final_kernel(*ins[:8], ins[8:], rest[:4], rest[4:8], rest[8], docs=docs, lo=lo, sizes=sizes, scale=scale)

        return pl.pallas_call(
            body,
            in_specs=[smem, smem] + [vmem] * (6 + len(parts)) + [hbm] * len(aliased),
            out_specs=[hbm] * 4,
            out_shape=[shaped(rows, width)] * 4,
            scratch_shapes=[pltpu.VMEM((rows, n * DH), BF16)] * 4 + [pltpu.SemaphoreType.DMA((len(sizes), 4))],
            input_output_aliases={first_alias + i: i for i in range(len(aliased))},
            compiler_params=params,
            cost_estimate=cost,
            name="final",
        )(dev, doc_blocks, *blocks, mine, other, *parts, *aliased)

    def across(x):
        return lax.ppermute(x, "seq", [(i, i ^ 1) for i in range(devices)])

    def along(x, by):
        pairs = [(i, i + by if i % 2 == 0 else i - by) for i in range(devices)]
        return lax.ppermute(x, "seq", [(i, j) for i, j in pairs if 0 <= j < devices])

    def plus(base, which, x):
        return pl.pallas_call(
            functools.partial(plus_kernel, which=which),
            in_specs=[smem] + [vmem] * 2,
            out_specs=vmem,
            out_shape=shaped(*base.shape),
            compiler_params=params,
            cost_estimate=cost,
            name="plus",
        )(flags, base, x)

    def close(near, far, keep):
        return pl.pallas_call(
            functools.partial(close_kernel, one=2, two=4),
            in_specs=[smem] + [vmem] * 3,
            out_specs=[vmem] * 2,
            out_shape=[shaped(*near.shape)] * 2,
            compiler_params=params,
            cost_estimate=cost,
            name="close",
        )(flags, near, far, keep)

    n_w = n_heads - N_X
    blocks, keep_x, send_x, flags = opened(N_X)
    keep_w, send_w = tails(blocks, N_X, n_w)
    total_x = plus(across(send_x), 0, keep_x)
    total_w = plus(across(send_w), 0, keep_w)
    near_x = along(total_x, 2)
    far_w = along(total_w, 4)
    part_w = local(blocks, N_X, n_w, 1024)
    far_w, part_w = lax.optimization_barrier((far_w, part_w))
    gathered_w = plus(total_w, 3, far_w)
    near_w = along(gathered_w, 2)
    later, _ = lax.optimization_barrier((blocks, gathered_w))
    part_x = local(later, 0, N_GAP, 1024)
    near_x, part_x = lax.optimization_barrier((near_x, part_x))
    gathered_x = plus(total_x, 1, near_x)
    far_x = along(gathered_x, 4)
    later, _ = lax.optimization_barrier((blocks, gathered_x))
    part_y = local(later, N_GAP, N_X - N_GAP, 10**10)
    far_x, part_y = lax.optimization_barrier((far_x, part_y))
    mine_x, pass_x = close(near_x, far_x, keep_x)
    mine_w, pass_w = close(near_w, far_w, keep_w)
    other_x = across(pass_x)
    other_w = across(pass_w)
    outs = final(blocks, 0, N_X, mine_x, other_x, (*part_x, *part_y), None)
    outs = final(blocks, N_X, n_w, mine_w, other_w, part_w, outs)
    return tuple(outs)


def solution(mesh):
    spec = P(("sweep", "seq"), None)
    return jax.shard_map(
        on_device,
        mesh=mesh,
        in_specs=(spec, spec, spec, spec, P("sweep")),
        out_specs=(spec, spec, spec, spec),
        check_vma=False,
    )
```

```python
import functools
import math

import jax
import jax.numpy as jnp
from jax import lax
from jax.experimental import pallas as pl
from jax.experimental.pallas import tpu as pltpu
from jax.sharding import PartitionSpec as P

DH = 128
UNIT = 128
LONGEST = 10
N_X = 18
EVEN = 5
F32 = jnp.float32
BF16 = jnp.bfloat16


def doc_of(pos, doc_ref, docs):
    count = jnp.int32(0)
    end = jnp.int32(0)
    for d in range(docs):
        end = end + doc_ref[d] * UNIT
        count = count + (pos >= end).astype(jnp.int32)
    return jnp.where(pos < 0, jnp.int32(-1), count)


def edges(pos_ref, doc_ref, rows, docs):
    first = pos_ref[0] * rows
    start = jnp.int32(0)
    stop = jnp.int32(1 << 30)
    end = jnp.int32(0)
    for d in range(docs):
        end = end + doc_ref[d] * UNIT
        start = jnp.where(end <= first + (rows - 1), end, start)
        stop = jnp.minimum(stop, jnp.where(end > first, end, jnp.int32(1 << 30)))
    return start - first, stop - first


def dot_tt(a, b):
    return lax.dot_general(a, b, (((0,), (0,)), ((), ())), preferred_element_type=F32)


def dot_nt(a, b):
    return lax.dot_general(a, b, (((1,), (1,)), ((), ())), preferred_element_type=F32)


def dot_nn(a, b):
    return lax.dot_general(a, b, (((1,), (0,)), ((), ())), preferred_element_type=F32)


def tails_of(q_ref, k_ref, v_ref, g_ref, flag_ref, rows_ref, keep_ref, send_ref, lo, sizes, ready=None):
    even = jnp.broadcast_to(flag_ref[EVEN : EVEN + 1, :], (DH, DH)) > 0
    at = 0
    for c, size in enumerate(sizes):
        if ready is not None:
            ready(c)
        for i in range(at, at + size):
            cols = pl.ds((lo + i) * DH, DH)
            tail = dot_tt(k_ref[:, cols] * rows_ref[0], v_ref[:, cols])
            head = dot_tt(q_ref[:, cols] * rows_ref[1], g_ref[:, cols])
            keep_ref[i] = jnp.where(even, tail, head).astype(BF16)
            send_ref[i] = jnp.where(even, head, tail).astype(BF16)
        at += size


def open_kernel(dev_ref, doc_hbm, q_hbm, k_hbm, v_hbm, g_hbm, q_ref, k_ref, v_ref, g_ref, keep_ref, send_ref, flag_ref, rows_ref, reach_ref, allowed_ref, doc_ref, doc_sem, sems, *, docs, sizes, scale):
    rows, width = q_ref.shape
    arrays = ((k_hbm, k_ref), (v_hbm, v_ref), (q_hbm, q_ref), (g_hbm, g_ref))
    rest = width // DH - sum(sizes)
    bounds = pltpu.make_async_copy(doc_hbm, doc_ref, doc_sem)
    bounds.start()
    copies = []
    at = 0
    for c, size in enumerate((*sizes, rest)):
        cols = pl.ds(at * DH, size * DH)
        group = [pltpu.make_async_copy(src.at[:, cols], dst.at[:, cols], sems.at[c, a]) for a, (src, dst) in enumerate(arrays)]
        for cp in group:
            cp.start()
        copies.append(group)
        at += size
    bounds.wait()
    dev = dev_ref[0]
    core = lax.rem(dev, 2)
    chip = dev - core
    first = dev * rows

    def key(u):
        pos = jnp.where(core == 0, rows * (chip + 2 - u) - 1, rows * (chip + u))
        return doc_of(pos, doc_ref, docs)

    k0, k1, k2, k4 = key(0), key(1), key(2), key(4)
    row = lax.broadcasted_iota(jnp.int32, (8, DH), 0)
    flags = jnp.zeros((8, DH), F32)
    for i, flag in enumerate((k1 == k0, k2 == k0, k4 == k2, k4 == k0, k2 == k1, core == 0)):
        flags = flags + jnp.where(row == i, flag.astype(F32), 0.0)
    flag_ref[...] = flags
    start, stop = edges(dev_ref, doc_ref, rows, docs)
    into = jnp.where(doc_of(first, doc_ref, docs) == doc_of(first - 1, doc_ref, docs), stop, 0)
    onto = jnp.where(doc_of(first + (rows - 1), doc_ref, docs) == doc_of(first + rows, doc_ref, docs), start, rows)
    row = lax.broadcasted_iota(jnp.int32, (rows, DH), 0)
    rows_ref[0] = jnp.where(row >= start, 1.0, 0.0).astype(BF16)
    rows_ref[1] = jnp.where(row < stop, 1.0, 0.0).astype(BF16)
    reach_ref[0] = jnp.where(row < into, scale, 0.0)
    reach_ref[1] = jnp.where(row >= onto, scale, 0.0)
    t = lax.broadcasted_iota(jnp.int32, (rows, rows), 0)
    s = lax.broadcasted_iota(jnp.int32, (rows, rows), 1)
    allowed_ref[...] = jnp.where((s <= t) & ((t < start) | (s >= start)), 1.0, 0.0).astype(BF16)

    def ready(c):
        for cp in copies[c]:
            cp.wait()

    tails_of(q_ref, k_ref, v_ref, g_ref, flag_ref, rows_ref, keep_ref, send_ref, 0, sizes, ready)
    ready(len(sizes))


def tails_kernel(q_ref, k_ref, v_ref, g_ref, flag_ref, rows_ref, keep_ref, send_ref, *, lo, n):
    tails_of(q_ref, k_ref, v_ref, g_ref, flag_ref, rows_ref, keep_ref, send_ref, lo, (n,))


def local_kernel(q_ref, k_ref, v_ref, g_ref, allowed_ref, o_ref, dq_ref, dk_ref, dv_ref, *, lo, n, scale, unroll):
    def step(j, carry):
        for u in range(unroll):
            i = j * unroll + u
            src = pl.ds(pl.multiple_of((lo + i) * DH, DH), DH)
            dst = pl.ds(pl.multiple_of(i * DH, DH), DH)
            q, k, v, g = q_ref[:, src], k_ref[:, src], v_ref[:, src], g_ref[:, src]
            probs = dot_nt(q, k).astype(BF16) * allowed_ref[...]
            dprobs = dot_nt(g, v).astype(BF16) * allowed_ref[...]
            o_ref[:, dst] = (scale * dot_nn(probs, v)).astype(BF16)
            dq_ref[:, dst] = (scale * dot_nn(dprobs, k)).astype(BF16)
            dk_ref[:, dst] = (scale * dot_tt(dprobs, q)).astype(BF16)
            dv_ref[:, dst] = (scale * dot_tt(probs, g)).astype(BF16)
        return carry

    lax.fori_loop(0, n // unroll, step, 0)


def final_kernel(q_ref, k_ref, v_ref, g_ref, flag_ref, reach_ref, mine_ref, other_ref, parts, outs, bufs, sems, *, lo, sizes):
    even = jnp.broadcast_to(flag_ref[EVEN : EVEN + 1, :], (DH, DH)) > 0
    copies = []
    at = 0
    for c, size in enumerate(sizes):
        for i in range(at, at + size):
            cols = pl.ds(i * DH, DH)
            src = pl.ds((lo + i) * DH, DH)
            q, k, v, g = q_ref[:, src], k_ref[:, src], v_ref[:, src], g_ref[:, src]
            mine, other = mine_ref[i].astype(F32), other_ref[i].astype(F32)
            state = jnp.where(even, mine, other).astype(BF16)
            back = jnp.where(even, other, mine).astype(BF16)
            terms = ((0, dot_nn(q, state)), (0, dot_nt(g, state)), (1, dot_nt(v, back)), (1, dot_nn(k, back)))
            for a, (side, term) in enumerate(terms):
                bufs[a][:, cols] = (parts[a][:, cols].astype(F32) + reach_ref[side] * term).astype(BF16)
        for a in range(4):
            cp = pltpu.make_async_copy(
                bufs[a].at[:, pl.ds(at * DH, size * DH)],
                outs[a].at[:, pl.ds((lo + at) * DH, size * DH)],
                sems.at[c, a],
            )
            cp.start()
            copies.append(cp)
        at += size
    for cp in copies:
        cp.wait()


def flag_of(flag_ref, which):
    return jnp.broadcast_to(flag_ref[which : which + 1, :], (DH, DH)).astype(BF16)


def plus_kernel(flag_ref, base_ref, x_ref, out_ref, *, which):
    flag = flag_of(flag_ref, which)
    for i in range(base_ref.shape[0]):
        out_ref[i] = base_ref[i] + flag * x_ref[i]


def close_kernel(flag_ref, near_ref, far_ref, keep_ref, mine_ref, pass_ref):
    flag, flag2 = flag_of(flag_ref, 2), flag_of(flag_ref, 4)
    for i in range(near_ref.shape[0]):
        mine = near_ref[i] + flag * far_ref[i]
        mine_ref[i] = mine
        pass_ref[i] = keep_ref[i] + flag2 * mine


def split(n, size):
    return (size,) * (n // size) + ((n % size,) if n % size else ())


def on_device(queries, keys, values, out_grad, doc_blocks):
    rows, width = queries.shape
    n_heads = width // DH
    docs = doc_blocks.shape[0]
    devices = lax.axis_size("seq")
    scale = 1.0 / math.sqrt(DH * n_heads * LONGEST)
    dev = lax.axis_index("seq").astype(jnp.int32).reshape(1)
    smem = pl.BlockSpec(memory_space=pltpu.SMEM)
    vmem = pl.BlockSpec(memory_space=pltpu.VMEM)
    hbm = pl.BlockSpec(memory_space=pltpu.HBM)
    params = pltpu.CompilerParams(vmem_limit_bytes=24 << 20)

    def shaped(*shape):
        return jax.ShapeDtypeStruct(shape, BF16)

    def call(body, ins, outs, name, flops=1024, **kw):
        return pl.pallas_call(
            body,
            in_specs=[vmem] * len(ins),
            out_specs=[vmem] * len(outs),
            out_shape=outs,
            compiler_params=params,
            cost_estimate=pl.CostEstimate(flops=flops, transcendentals=0, bytes_accessed=1024),
            name=name,
        )(*ins)

    def opened(n):
        sizes = split(n, 4)
        out = pl.pallas_call(
            functools.partial(open_kernel, docs=docs, sizes=sizes, scale=scale),
            in_specs=[smem] + [hbm] * 5,
            out_specs=[vmem] * 10,
            out_shape=[shaped(rows, width)] * 4
            + [shaped(n, DH, DH)] * 2
            + [jax.ShapeDtypeStruct((8, DH), F32), shaped(2, rows, DH), jax.ShapeDtypeStruct((2, rows, DH), F32), shaped(rows, rows)],
            scratch_shapes=[pltpu.SMEM((docs,), jnp.int32), pltpu.SemaphoreType.DMA, pltpu.SemaphoreType.DMA((len(sizes) + 1, 4))],
            compiler_params=params,
            cost_estimate=pl.CostEstimate(flops=1000, transcendentals=0, bytes_accessed=1024),
            name="opened",
        )(dev, *(pltpu.with_memory_space_constraint(x, pltpu.HBM) for x in (doc_blocks, queries, keys, values, out_grad)))
        return out[:4], out[4], out[5], out[6:]

    def tails(lo, n):
        body = functools.partial(tails_kernel, lo=lo, n=n)
        return call(body, (*blocks, flags, edge_rows), [shaped(n, DH, DH)] * 2, "tails", 1000000000)

    def local(blocks, lo, n, flops):
        body = functools.partial(local_kernel, lo=lo, n=n, scale=scale, unroll=2)
        return call(body, (*blocks, allowed), [shaped(rows, n * DH)] * 4, "local", flops)

    def final(lo, n, mine, other, parts, outs):
        aliased = [] if outs is None else list(outs)
        sizes = split(n, 4)

        def body(*refs):
            ins, rest = refs[:12], refs[12 + len(aliased) :]
            final_kernel(*ins[:8], ins[8:], rest[:4], rest[4:8], rest[8], lo=lo, sizes=sizes)

        return pl.pallas_call(
            body,
            in_specs=[vmem] * 12 + [hbm] * len(aliased),
            out_specs=[hbm] * 4,
            out_shape=[shaped(rows, width)] * 4,
            scratch_shapes=[pltpu.VMEM((rows, n * DH), BF16)] * 4 + [pltpu.SemaphoreType.DMA((len(sizes), 4))],
            input_output_aliases={12 + i: i for i in range(len(aliased))},
            compiler_params=params,
            cost_estimate=pl.CostEstimate(flops=1000000000, transcendentals=0, bytes_accessed=1024),
            name="final",
        )(*blocks, flags, reach, mine, other, *parts, *aliased)

    def across(x):
        return lax.ppermute(x, "seq", [(i, i ^ 1) for i in range(devices)])

    def along(x, by):
        pairs = [(i, i + by if i % 2 == 0 else i - by) for i in range(devices)]
        return lax.ppermute(x, "seq", [(i, j) for i, j in pairs if 0 <= j < devices])

    def plus(base, which, x):
        return call(functools.partial(plus_kernel, which=which), (flags, base, x), [shaped(*base.shape)], "plus", 1000000000)[0]

    def close(near, far, keep):
        return call(close_kernel, (flags, near, far, keep), [shaped(*near.shape)] * 2, "close", 10000000000)

    n_w = n_heads - N_X
    blocks, keep_x, send_x, (flags, edge_rows, reach, allowed) = opened(N_X)
    keep_w, send_w = tails(N_X, n_w)
    total_x = plus(across(send_x), 0, keep_x)
    total_w = plus(across(send_w), 0, keep_w)
    near_x = along(total_x, 2)
    far_w = along(total_w, 4)
    part_w = local(blocks, N_X, n_w, 1000000000)
    far_w, part_w = lax.optimization_barrier((far_w, part_w))
    gathered_w = plus(total_w, 3, far_w)
    near_w = along(gathered_w, 2)
    near_x, _ = lax.optimization_barrier((near_x, gathered_w))
    gathered_x = plus(total_x, 1, near_x)
    far_x = along(gathered_x, 4)
    later, _ = lax.optimization_barrier((blocks, gathered_x))
    part_x = local(later, 0, N_X, 10000000000)
    far_x, part_x = lax.optimization_barrier((far_x, part_x))
    mine_x, pass_x = close(near_x, far_x, keep_x)
    other_x = across(pass_x)
    outs = final(0, N_X, mine_x, other_x, part_x, None)
    near_w, _ = lax.optimization_barrier((near_w, pass_x))
    mine_w, pass_w = close(near_w, far_w, keep_w)
    other_w = across(pass_w)
    outs = final(N_X, n_w, mine_w, other_w, part_w, outs)
    return tuple(outs)


def solution(mesh):
    spec = P(("sweep", "seq"), None)
    return jax.shard_map(
        on_device,
        mesh=mesh,
        in_specs=(spec, spec, spec, spec, P("sweep")),
        out_specs=(spec, spec, spec, spec),
        check_vma=False,
    )
```

```python
import functools
import math

import jax
import jax.numpy as jnp
from jax import lax
from jax.experimental import pallas as pl
from jax.experimental.pallas import tpu as pltpu
from jax.sharding import PartitionSpec as P

DH = 128
UNIT = 128
LONGEST = 10
N_X = 18
EVEN = 5
F32 = jnp.float32
BF16 = jnp.bfloat16


def doc_of(pos, doc_ref, docs):
    count = jnp.int32(0)
    end = jnp.int32(0)
    for d in range(docs):
        end = end + doc_ref[d] * UNIT
        count = count + (pos >= end).astype(jnp.int32)
    return jnp.where(pos < 0, jnp.int32(-1), count)


def edges(pos_ref, doc_ref, rows, docs):
    first = pos_ref[0] * rows
    start = jnp.int32(0)
    stop = jnp.int32(1 << 30)
    end = jnp.int32(0)
    for d in range(docs):
        end = end + doc_ref[d] * UNIT
        start = jnp.where(end <= first + (rows - 1), end, start)
        stop = jnp.minimum(stop, jnp.where(end > first, end, jnp.int32(1 << 30)))
    return start - first, stop - first


def dot_tt(a, b):
    return lax.dot_general(a, b, (((0,), (0,)), ((), ())), preferred_element_type=F32)


def dot_nt(a, b):
    return lax.dot_general(a, b, (((1,), (1,)), ((), ())), preferred_element_type=F32)


def dot_nn(a, b):
    return lax.dot_general(a, b, (((1,), (0,)), ((), ())), preferred_element_type=F32)


def tails_of(q_ref, k_ref, v_ref, g_ref, flag_ref, rows_ref, keep_ref, send_ref, lo, sizes, ready=None):
    even = jnp.broadcast_to(flag_ref[EVEN : EVEN + 1, :], (DH, DH)) > 0
    at = 0
    for c, size in enumerate(sizes):
        if ready is not None:
            ready(c)
        for i in range(at, at + size):
            cols = pl.ds((lo + i) * DH, DH)
            tail = dot_tt(k_ref[:, cols] * rows_ref[0], v_ref[:, cols])
            head = dot_tt(q_ref[:, cols] * rows_ref[1], g_ref[:, cols])
            keep_ref[i] = jnp.where(even, tail, head).astype(BF16)
            send_ref[i] = jnp.where(even, head, tail).astype(BF16)
        at += size


def open_kernel(dev_ref, doc_hbm, q_hbm, k_hbm, v_hbm, g_hbm, q_ref, k_ref, v_ref, g_ref, keep_ref, send_ref, flag_ref, rows_ref, reach_ref, allowed_ref, turned_ref, doc_ref, doc_sem, sems, *, docs, sizes, scale):
    rows, width = q_ref.shape
    arrays = ((k_hbm, k_ref), (v_hbm, v_ref), (q_hbm, q_ref), (g_hbm, g_ref))
    rest = width // DH - sum(sizes)
    bounds = pltpu.make_async_copy(doc_hbm, doc_ref, doc_sem)
    bounds.start()
    copies = []
    at = 0
    for c, size in enumerate((*sizes, rest)):
        cols = pl.ds(at * DH, size * DH)
        group = [pltpu.make_async_copy(src.at[:, cols], dst.at[:, cols], sems.at[c, a]) for a, (src, dst) in enumerate(arrays)]
        for cp in group:
            cp.start()
        copies.append(group)
        at += size
    bounds.wait()
    dev = dev_ref[0]
    core = lax.rem(dev, 2)
    chip = dev - core
    first = dev * rows

    def key(u):
        pos = jnp.where(core == 0, rows * (chip + 2 - u) - 1, rows * (chip + u))
        return doc_of(pos, doc_ref, docs)

    k0, k1, k2, k4 = key(0), key(1), key(2), key(4)
    row = lax.broadcasted_iota(jnp.int32, (8, DH), 0)
    flags = jnp.zeros((8, DH), F32)
    for i, flag in enumerate((k1 == k0, k2 == k0, k4 == k2, k4 == k0, k2 == k1, core == 0)):
        flags = flags + jnp.where(row == i, flag.astype(F32), 0.0)
    flag_ref[...] = flags
    start, stop = edges(dev_ref, doc_ref, rows, docs)
    into = jnp.where(doc_of(first, doc_ref, docs) == doc_of(first - 1, doc_ref, docs), stop, 0)
    onto = jnp.where(doc_of(first + (rows - 1), doc_ref, docs) == doc_of(first + rows, doc_ref, docs), start, rows)
    row = lax.broadcasted_iota(jnp.int32, (rows, DH), 0)
    rows_ref[0] = jnp.where(row >= start, 1.0, 0.0).astype(BF16)
    rows_ref[1] = jnp.where(row < stop, 1.0, 0.0).astype(BF16)
    reach_ref[0] = jnp.where(row < into, scale, 0.0)
    reach_ref[1] = jnp.where(row >= onto, scale, 0.0)
    t = lax.broadcasted_iota(jnp.int32, (rows, rows), 0)
    s = lax.broadcasted_iota(jnp.int32, (rows, rows), 1)
    allowed_ref[...] = jnp.where((s <= t) & ((t < start) | (s >= start)), 1.0, 0.0).astype(BF16)
    turned_ref[...] = jnp.where((t <= s) & ((s < start) | (t >= start)), 1.0, 0.0).astype(BF16)

    def ready(c):
        for cp in copies[c]:
            cp.wait()

    tails_of(q_ref, k_ref, v_ref, g_ref, flag_ref, rows_ref, keep_ref, send_ref, 0, sizes, ready)
    ready(len(sizes))


def tails_kernel(q_ref, k_ref, v_ref, g_ref, flag_ref, rows_ref, keep_ref, send_ref, *, lo, n):
    tails_of(q_ref, k_ref, v_ref, g_ref, flag_ref, rows_ref, keep_ref, send_ref, lo, (n,))


def local_kernel(q_ref, k_ref, v_ref, g_ref, allowed_ref, turned_ref, o_ref, dq_ref, dk_ref, dv_ref, *, lo, n, scale, unroll):
    def step(j, carry):
        for u in range(unroll):
            i = j * unroll + u
            src = pl.ds(pl.multiple_of((lo + i) * DH, DH), DH)
            dst = pl.ds(pl.multiple_of(i * DH, DH), DH)
            q, k, v, g = q_ref[:, src], k_ref[:, src], v_ref[:, src], g_ref[:, src]
            probs = dot_nt(q, k).astype(BF16) * allowed_ref[...]
            dprobs = dot_nt(g, v).astype(BF16) * allowed_ref[...]
            probs_t = dot_nt(k, q).astype(BF16) * turned_ref[...]
            dprobs_t = dot_nt(v, g).astype(BF16) * turned_ref[...]
            o_ref[:, dst] = (scale * dot_nn(probs, v)).astype(BF16)
            dq_ref[:, dst] = (scale * dot_nn(dprobs, k)).astype(BF16)
            dk_ref[:, dst] = (scale * dot_nn(dprobs_t, q)).astype(BF16)
            dv_ref[:, dst] = (scale * dot_nn(probs_t, g)).astype(BF16)
        return carry

    lax.fori_loop(0, n // unroll, step, 0)


def final_kernel(q_ref, k_ref, v_ref, g_ref, flag_ref, reach_ref, shares, outs, bufs, pair_ref, sems, *, chunks):
    even = jnp.broadcast_to(flag_ref[EVEN : EVEN + 1, :], (DH, DH)) > 0
    pair_ref[...] = jnp.zeros_like(pair_ref)
    copies = []
    at = 0
    for c, (share, size) in enumerate(chunks):
        mine_ref, other_ref, *parts = shares[share]
        base = 0 if share == 0 else shares[0][0].shape[0]
        for i in range(at, at + size, 2):
            slot = 2 * ((i // 2) % 2)
            for u in range(2):
                mine, other = mine_ref[i + u - base].astype(F32), other_ref[i + u - base].astype(F32)
                own = pl.ds(u * DH, DH)
                pair_ref[slot, own, own] = jnp.where(even, mine, other).astype(BF16)
                pair_ref[slot + 1, own, own] = jnp.where(even, other, mine).astype(BF16)
            src = pl.ds(i * DH, 2 * DH)
            state, back = pair_ref[slot], pair_ref[slot + 1]
            terms = ((0, dot_nn(q_ref[:, src], state)), (0, dot_nt(g_ref[:, src], state)), (1, dot_nt(v_ref[:, src], back)), (1, dot_nn(k_ref[:, src], back)))
            for a, (side, term) in enumerate(terms):
                for u in range(2):
                    inner = pl.ds((i + u - base) * DH, DH)
                    piece = parts[a][:, inner].astype(F32) + reach_ref[side] * term[:, u * DH : (u + 1) * DH]
                    bufs[a][:, pl.ds((i + u) * DH, DH)] = piece.astype(BF16)
        cols = pl.ds(at * DH, size * DH)
        for a in range(4):
            cp = pltpu.make_async_copy(bufs[a].at[:, cols], outs[a].at[:, cols], sems.at[c, a])
            cp.start()
            copies.append(cp)
        at += size
    for cp in copies:
        cp.wait()


def flag_of(flag_ref, which):
    return jnp.broadcast_to(flag_ref[which : which + 1, :], (DH, DH)).astype(BF16)


def plus_kernel(flag_ref, base_ref, x_ref, out_ref, *, which):
    flag = flag_of(flag_ref, which)
    for i in range(base_ref.shape[0]):
        out_ref[i] = base_ref[i] + flag * x_ref[i]


def close_kernel(flag_ref, near_ref, far_ref, keep_ref, mine_ref, pass_ref):
    flag, flag2 = flag_of(flag_ref, 2), flag_of(flag_ref, 4)
    for i in range(near_ref.shape[0]):
        mine = near_ref[i] + flag * far_ref[i]
        mine_ref[i] = mine
        pass_ref[i] = keep_ref[i] + flag2 * mine


def split(n, size):
    return (size,) * (n // size) + ((n % size,) if n % size else ())


def on_device(queries, keys, values, out_grad, doc_blocks):
    rows, width = queries.shape
    n_heads = width // DH
    docs = doc_blocks.shape[0]
    devices = lax.axis_size("seq")
    scale = 1.0 / math.sqrt(DH * n_heads * LONGEST)
    dev = lax.axis_index("seq").astype(jnp.int32).reshape(1)
    smem = pl.BlockSpec(memory_space=pltpu.SMEM)
    vmem = pl.BlockSpec(memory_space=pltpu.VMEM)
    hbm = pl.BlockSpec(memory_space=pltpu.HBM)
    params = pltpu.CompilerParams(vmem_limit_bytes=24 << 20)

    def shaped(*shape):
        return jax.ShapeDtypeStruct(shape, BF16)

    def call(body, ins, outs, name, flops=1024, **kw):
        return pl.pallas_call(
            body,
            in_specs=[vmem] * len(ins),
            out_specs=[vmem] * len(outs),
            out_shape=outs,
            compiler_params=params,
            cost_estimate=pl.CostEstimate(flops=flops, transcendentals=0, bytes_accessed=1024),
            name=name,
        )(*ins)

    def opened(n):
        sizes = split(n, 4)
        out = pl.pallas_call(
            functools.partial(open_kernel, docs=docs, sizes=sizes, scale=scale),
            in_specs=[smem] + [hbm] * 5,
            out_specs=[vmem] * 11,
            out_shape=[shaped(rows, width)] * 4
            + [shaped(n, DH, DH)] * 2
            + [jax.ShapeDtypeStruct((8, DH), F32), shaped(2, rows, DH), jax.ShapeDtypeStruct((2, rows, DH), F32)]
            + [shaped(rows, rows)] * 2,
            scratch_shapes=[pltpu.SMEM((docs,), jnp.int32), pltpu.SemaphoreType.DMA, pltpu.SemaphoreType.DMA((len(sizes) + 1, 4))],
            compiler_params=params,
            cost_estimate=pl.CostEstimate(flops=1000, transcendentals=0, bytes_accessed=1024),
            name="opened",
        )(dev, *(pltpu.with_memory_space_constraint(x, pltpu.HBM) for x in (doc_blocks, queries, keys, values, out_grad)))
        return out[:4], out[4], out[5], out[6:]

    def tails(lo, n):
        body = functools.partial(tails_kernel, lo=lo, n=n)
        return call(body, (*blocks, flags, edge_rows), [shaped(n, DH, DH)] * 2, "tails", 1000000000)

    def local(blocks, lo, n, flops):
        body = functools.partial(local_kernel, lo=lo, n=n, scale=scale, unroll=max(u for u in range(1, 7) if n % u == 0))
        return call(body, (*blocks, *allowed), [shaped(rows, n * DH)] * 4, "local", flops)

    def final(share_x, share_w):
        def chunked(n):
            return split(n - 2, 4) + (2,)

        chunks = [(0, size) for size in chunked(share_x[0].shape[0])] + [(1, size) for size in chunked(share_w[0].shape[0])]

        def body(*refs):
            shares = (refs[6:12], refs[12:18])
            final_kernel(*refs[:6], shares, refs[18:22], refs[22:26], *refs[26:], chunks=chunks)

        return pl.pallas_call(
            body,
            in_specs=[vmem] * 18,
            out_specs=[hbm] * 4,
            out_shape=[shaped(rows, width)] * 4,
            scratch_shapes=[pltpu.VMEM((rows, width), BF16)] * 4 + [pltpu.VMEM((4, 2 * DH, 2 * DH), BF16), pltpu.SemaphoreType.DMA((len(chunks), 4))],
            compiler_params=params,
            cost_estimate=pl.CostEstimate(flops=1000000000, transcendentals=0, bytes_accessed=1024),
            name="final",
        )(*blocks, flags, reach, *share_x, *share_w)

    def across(x):
        return lax.ppermute(x, "seq", [(i, i ^ 1) for i in range(devices)])

    def along(x, by):
        pairs = [(i, i + by if i % 2 == 0 else i - by) for i in range(devices)]
        return lax.ppermute(x, "seq", [(i, j) for i, j in pairs if 0 <= j < devices])

    def plus(base, which, x):
        return call(functools.partial(plus_kernel, which=which), (flags, base, x), [shaped(*base.shape)], "plus", 1000000000)[0]

    def close(near, far, keep):
        return call(close_kernel, (flags, near, far, keep), [shaped(*near.shape)] * 2, "close", 10000000000)

    n_w = n_heads - N_X
    blocks, keep_x, send_x, (flags, edge_rows, reach, *allowed) = opened(N_X)
    keep_w, send_w = tails(N_X, n_w)
    total_x = plus(across(send_x), 0, keep_x)
    total_w = plus(across(send_w), 0, keep_w)
    near_x = along(total_x, 2)
    far_w = along(total_w, 4)
    part_w = local(blocks, N_X, n_w, 1000000000)
    far_w, part_w = lax.optimization_barrier((far_w, part_w))
    gathered_w = plus(total_w, 3, far_w)
    near_w = along(gathered_w, 2)
    near_x, _ = lax.optimization_barrier((near_x, gathered_w))
    gathered_x = plus(total_x, 1, near_x)
    far_x = along(gathered_x, 4)
    later, _ = lax.optimization_barrier((blocks, gathered_x))
    part_x = local(later, 0, N_X, 10000000000)
    far_x, part_x = lax.optimization_barrier((far_x, part_x))
    mine_x, pass_x = close(near_x, far_x, keep_x)
    near_w, _ = lax.optimization_barrier((near_w, pass_x))
    mine_w, pass_w = close(near_w, far_w, keep_w)
    other_x = across(pass_x)
    other_w = across(pass_w)
    outs = final((mine_x, other_x, *part_x), (mine_w, other_w, *part_w))
    return tuple(outs)


def solution(mesh):
    spec = P(("sweep", "seq"), None)
    return jax.shard_map(
        on_device,
        mesh=mesh,
        in_specs=(spec, spec, spec, spec, P("sweep")),
        out_specs=(spec, spec, spec, spec),
        check_vma=False,
    )
```
